256 devices in a mesh: layer: 8 (over y, core), blk: 32 (over x, z).
Axes of the slice: x: 4, y: 4, z: 8, core: 2. Of those that a mesh axis runs over, the one named last changes fastest.
Arguments:
- source: bfloat16 [8, 2, 128, 32768], P('layer', None, None, 'blk'), may hold values from -6 to 6
- tile_data: bfloat16 [8, 192, 2, 512, 512], P('layer', 'blk'), may hold values from -0.078125 to 0.078125
- tile_rows: int32 [8, 192], P('layer', 'blk'), may hold values from 0 to 63, as said below
- tile_cols: int32 [8, 192], P('layer', 'blk'), may hold values from 0 to 63, as said below
- tile_count: int32 [8, 32], P('layer', 'blk'), may hold values from 4 to 6, as said below
Outputs:
- down_trace: bfloat16 [8, 2, 128, 32768], P('layer', None, None, 'blk')
- up_trace: bfloat16 [8, 2, 128, 32768], P('layer', None, None, 'blk')
The draws below stay inside these ranges and needn't reach their ends.
Inputs may be any that keep to these rules, and one draw needn't show every extreme that they name: `tile_rows`: every slot of row range g (slots g*6 to (g+1)*6 - 1) has its row block in g*2 to (g+1)*2 - 1; the live slots of one range hold distinct tiles in shuffled order, among them the diagonal tile of each of its row blocks, and the tile one block left of its first row block and one block right of its last where those exist. Slots that are not live also hold valid indices. `tile_cols`: every slot's column block lies within 2 blocks of its row block, inside the grid. `tile_count`: in every section some row range has all 6 slots live.
All inputs are finite; a program needn't handle non-finite values.
Results may differ from the reference program's by a relative error of at most 0.01.
Values may be sent and summed in bfloat16 or wider, within the bound.
No kernel may reach another device: no remote copies, remote signals or barrier semaphores. Data moves between devices by JAX's collectives and lax.ppermute only.
A program may use at most 64 MiB of HBM per device.

```python
import jax
import jax.numpy as jnp
from jax import lax

TILE = 512
ROWS = 32768
BAND = 2
LAYERS = 8
COLS = 128
ROW_BLOCKS = 64
RB_DEV = 2
SLOTS = 6
N_LAYER = 8
N_BLK = 32


def tile_lists(key):
    groups = ROW_BLOCKS // RB_DEV
    cand_n = 4 * RB_DEV
    offsets = jnp.array([-2, -1, 1, 2], jnp.int32)
    group_ids = jnp.arange(groups, dtype=jnp.int32)
    own_rows = group_ids[:, None] * RB_DEV + jnp.arange(RB_DEV, dtype=jnp.int32)[None, :]
    cand_rows = jnp.repeat(own_rows, 4, axis=1)
    offset_all = jnp.tile(offsets, RB_DEV)
    local_pos = jnp.repeat(jnp.arange(RB_DEV, dtype=jnp.int32), 4)
    cand_cols = cand_rows + offset_all[None, :]
    usable = (cand_cols >= 0) & (cand_cols < ROW_BLOCKS)
    forced = usable & ((local_pos == 0) & (offset_all == -1) | (local_pos == RB_DEV - 1) & (offset_all == 1))[None, :]
    subkeys = jax.random.split(jax.random.fold_in(key, 7), 4)
    jitter = jax.random.randint(subkeys[0], (N_LAYER, groups, cand_n), 0, 1 << 16)
    ranking = jnp.where(forced[None], 0, jnp.where(usable[None], 1 + jitter, 1 << 17))
    ordering = jnp.argsort(ranking * cand_n + jnp.arange(cand_n, dtype=jnp.int32), axis=-1)
    extra_n = SLOTS - RB_DEV
    picked = ordering[..., :extra_n]
    wide_rows = jnp.broadcast_to(cand_rows[None], (N_LAYER, groups, cand_n))
    wide_cols = jnp.broadcast_to(cand_cols[None], (N_LAYER, groups, cand_n))
    extra_rows = jnp.take_along_axis(wide_rows, picked, axis=-1)
    extra_cols = jnp.take_along_axis(wide_cols, picked, axis=-1)
    diag_rows = jnp.broadcast_to(own_rows[None], (N_LAYER, groups, RB_DEV))
    slot_rows = jnp.concatenate([diag_rows, extra_rows], axis=-1)
    slot_cols = jnp.concatenate([diag_rows, extra_cols], axis=-1)
    counts = jax.random.randint(subkeys[1], (N_LAYER, groups), RB_DEV + 2, SLOTS + 1)
    fullest = jax.random.randint(subkeys[2], (N_LAYER, 1), 0, groups)
    counts = jnp.where(group_ids[None, :] == fullest, SLOTS, counts).astype(jnp.int32)
    slot_pos = jnp.arange(SLOTS, dtype=jnp.int32)
    shuffle_jitter = jax.random.randint(subkeys[3], (N_LAYER, groups, SLOTS), 0, 1 << 16)
    shuffle_rank = jnp.where(slot_pos[None, None, :] < counts[..., None], shuffle_jitter, (1 << 17) + slot_pos[None, None, :])
    shuffle = jnp.argsort(shuffle_rank * SLOTS + slot_pos[None, None, :], axis=-1)
    slot_rows = jnp.take_along_axis(slot_rows, shuffle, axis=-1)
    slot_cols = jnp.take_along_axis(slot_cols, shuffle, axis=-1)
    return (slot_rows.reshape(N_LAYER, groups * SLOTS).astype(jnp.int32), slot_cols.reshape(N_LAYER, groups * SLOTS).astype(jnp.int32), counts)


def draw_tile_rows(key, part):
    return tile_lists(key)[0]


def draw_tile_cols(key, part):
    return tile_lists(key)[1]


def draw_tile_count(key, part):
    return tile_lists(key)[2]


def block_scale(rng, shape, cuts, least, high):
    def one(position, blocks):
        steps = jax.random.uniform(jax.random.fold_in(jax.random.fold_in(rng, 6), position), (blocks,), jnp.float32, least / len(cuts), high / len(cuts))
        return jnp.repeat(jnp.exp(steps), shape[position] // blocks).reshape((-1,) + (1,) * (len(shape) - position - 1))

    level = one(*cuts[0])
    for cut in cuts[1:]:
        level = level * one(*cut)
    return level


def normal_values(rng, shape, deviation, most, cuts=(), held_as=jnp.bfloat16):
    drawn = deviation * jax.random.normal(rng, shape, jnp.float32)
    if cuts:
        drawn = drawn * block_scale(rng, shape, cuts, -0.22, 0.18)
    return jnp.clip(drawn, -most, most).astype(held_as)


def setup_inputs(seed: int = 0) -> dict:
    keys = jax.random.split(jax.random.key(seed), 6)
    source = normal_values(keys[0], (LAYERS, 2, COLS, ROWS), 1.0, 6.0, ((0, 8), (3, 32)))
    tile_data = normal_values(keys[1], (LAYERS, N_BLK * SLOTS, 2, TILE, TILE), (12 * TILE) ** -0.5, 0.078125, ((0, 8), (1, 32)))
    tile_rows = draw_tile_rows(jax.random.fold_in(keys[5], 71), 0)
    tile_cols = draw_tile_cols(jax.random.fold_in(keys[5], 71), 0)
    tile_count = draw_tile_count(jax.random.fold_in(keys[5], 71), 0)
    return dict(source=source, tile_data=tile_data, tile_rows=tile_rows, tile_cols=tile_cols, tile_count=tile_count)


def complex_apply(segment, matrix, contract):
    halves = segment.shape[1]
    flattened = segment.reshape(2 * halves, segment.shape[2])
    numbers = (((1,), (contract,)), ((), ()))
    with_real = lax.dot_general(flattened, matrix[0], numbers, precision=lax.Precision.HIGHEST, preferred_element_type=jnp.float32)
    with_imag = lax.dot_general(flattened, matrix[1], numbers, precision=lax.Precision.HIGHEST, preferred_element_type=jnp.float32)
    return jnp.stack((with_real[:halves] - with_imag[halves:], with_imag[:halves] + with_real[halves:]))


def live_slots(tile_count, layer_index):
    groups = tile_count.shape[1]
    slot_ids = jnp.arange(groups * SLOTS, dtype=jnp.int32)
    return (slot_ids % SLOTS) < jnp.repeat(tile_count[layer_index], SLOTS)


def apply_down(tile_layer, rows_layer, cols_layer, usable, current):
    values = current.astype(jnp.float32)

    def one_slot(summed, inputs):
        matrix, row_block, col_block, is_live = inputs
        segment = lax.dynamic_slice_in_dim(values, col_block * TILE, TILE, 2)
        product = complex_apply(segment, matrix.astype(jnp.float32), 1)
        start_row = row_block * TILE
        target = lax.dynamic_slice_in_dim(summed, start_row, TILE, 2)
        return lax.dynamic_update_slice_in_dim(summed, target + jnp.where(is_live, product, 0.0), start_row, 2), None

    summed, ignored = lax.scan(one_slot, jnp.zeros(values.shape, jnp.float32), (tile_layer, rows_layer, cols_layer, usable))
    return summed


def apply_up(tile_layer, rows_layer, cols_layer, usable, current):
    groups = rows_layer.shape[0] // SLOTS
    rows_dev = ROWS // groups
    margin = BAND * TILE
    values = current.astype(jnp.float32)
    columns = values.shape[1]
    positions = jnp.arange(rows_dev + 2 * margin, dtype=jnp.int32)
    inside = (positions >= margin) & (positions < margin + rows_dev)

    def one_group(padded, inputs):
        group_tiles, group_rows, group_cols, group_live, group_index = inputs
        first_row = group_index * rows_dev

        def one_slot(extended, slot_inputs):
            matrix, row_block, col_block, is_live = slot_inputs
            segment = lax.dynamic_slice_in_dim(values, row_block * TILE, TILE, 2)
            product = complex_apply(segment, matrix.astype(jnp.float32), 0)
            placed_at = col_block * TILE - first_row + margin
            target = lax.dynamic_slice_in_dim(extended, placed_at, TILE, 2)
            return lax.dynamic_update_slice_in_dim(extended, target + jnp.where(is_live, product, 0.0), placed_at, 2), None

        extended, ignored = lax.scan(one_slot, jnp.zeros((2, columns, rows_dev + 2 * margin), jnp.float32), (group_tiles, group_rows, group_cols, group_live))
        narrowed = lax.optimization_barrier(extended.astype(jnp.bfloat16)).astype(jnp.float32)
        shared = jnp.where(inside, extended, narrowed)
        target = lax.dynamic_slice_in_dim(padded, first_row, rows_dev + 2 * margin, 2)
        return lax.dynamic_update_slice_in_dim(padded, target + shared, first_row, 2), None

    padded, ignored = lax.scan(
        one_group,
        jnp.zeros((2, columns, ROWS + 2 * margin), jnp.float32),
        (tile_layer.reshape(groups, SLOTS, 2, TILE, TILE), rows_layer.reshape(groups, SLOTS), cols_layer.reshape(groups, SLOTS), usable.reshape(groups, SLOTS), jnp.arange(groups, dtype=jnp.int32)),
    )
    return padded[:, :, margin:margin + ROWS]


def reference(source, tile_data, tile_rows, tile_cols, tile_count):
    down_list = []
    forward = None
    for layer_index in range(N_LAYER):
        if layer_index == 0:
            current = source[0]
        else:
            current = (source[layer_index].astype(jnp.float32) + forward.astype(jnp.float32)).astype(jnp.bfloat16)
        down_list.append(current)
        if layer_index + 1 < N_LAYER:
            forward = apply_down(tile_data[layer_index], tile_rows[layer_index], tile_cols[layer_index], live_slots(tile_count, layer_index), current).astype(jnp.bfloat16)
    up_list = [None] * N_LAYER
    backward = None
    for layer_index in reversed(range(N_LAYER)):
        if layer_index == N_LAYER - 1:
            current = down_list[layer_index]
        else:
            current = (down_list[layer_index].astype(jnp.float32) + backward.astype(jnp.float32)).astype(jnp.bfloat16)
        up_list[layer_index] = current
        if layer_index > 0:
            backward = apply_up(tile_data[layer_index], tile_rows[layer_index], tile_cols[layer_index], live_slots(tile_count, layer_index), current).astype(jnp.bfloat16)
    return jnp.stack(down_list), jnp.stack(up_list)
```

```python
import functools

import jax
import jax.numpy as jnp
from jax import lax
from jax.experimental import pallas as pl
from jax.experimental.pallas import tpu as pltpu
from jax.sharding import PartitionSpec as P

WAVES = 2
PITCH = 3
ORDER = (0, 1, -1)
AXES = ("layer", "blk")
F32, BF16 = jnp.float32, jnp.bfloat16
META = 4


def schedule(layers):
    top = layers - 1
    steps = []
    for step in range(2 * top + 1 + PITCH * (WAVES - 1)):
        waves = []
        for b in range(WAVES):
            t = step - PITCH * b
            if 0 <= t < top:
                waves.append((b, t, 1, t))
            elif top <= t < 2 * top:
                waves.append((b, 2 * top - t, 3 if t == top else 2, 2 * top - t - 1))
            elif t == 2 * top:
                waves.append((b, 0, 4, None))
        steps.append(waves)
    return steps


def route(hops, shift, layers, ranges):
    to = {i: i for i in range(layers * ranges)}
    for k in hops:
        for g in range(max(0, -shift), ranges - max(0, shift)):
            a, b = k * ranges + g, (k + 1) * ranges + g + shift
            to[a], to[b] = b, a
    return sorted(to.items())


def stacked(real, imag):
    return jnp.concatenate(
        [jnp.concatenate([real, imag], axis=0), jnp.concatenate([-imag, real], axis=0)], axis=1
    )


def step_kernel(waves, has_halo, meta, tiles, here, left, right, below, down_in, up_in, *rest):
    downs = [w for w in waves if w[2] == 1]
    ups = [w for w in waves if w[2] != 1]
    if has_halo:
        halo_l, halo_r, *rest = rest
    n_send = 3 if ups else 1
    sends, (down_all, up_all, lhs, acc) = rest[:n_send], rest[n_send:]
    shots = here.shape[1]
    tile = tiles.shape[2]
    layer, count = meta[0], meta[1]
    slots = (meta.shape[0] - META) // 2
    mode, wave = jnp.int32(0), jnp.int32(0)
    for b, at, code, _ in waves:
        mode = jnp.where(layer == at, code, mode)
        wave = jnp.where(layer == at, b, wave)
    mine = pl.ds(pl.multiple_of(wave * shots, shots), shots)

    def product(slot, source, contract):
        numbers = (((1,), (contract,)), ((), ()))
        x = lhs[source]
        return lax.dot_general(x[:, :tile], tiles[slot, 0], numbers, preferred_element_type=F32) + (
            lax.dot_general(x[:, tile:], tiles[slot, 1], numbers, preferred_element_type=F32)
        )

    def fill(index, ref, rows=slice(None)):
        for j in range(2):
            piece = slice(j * tile, (j + 1) * tile)
            lhs[index + j] = stacked(ref[0, rows, piece], ref[1, rows, piece])

    def next_down():
        fill(0, left)
        fill(2, here)
        fill(4, right)
        down_all[0, mine, :] = here[0]
        down_all[1, mine, :] = here[1]

    def first():
        fill(0, halo_l)
        fill(2, down_all, mine)
        fill(4, halo_r)

    def down():
        for j in range(2):
            acc[j] = jnp.zeros(acc.shape[1:], F32)

        def one(slot, carry):
            acc[meta[META + slot]] += product(slot, meta[META + slots + slot], 1)
            return carry

        lax.fori_loop(0, count, one, 0)
        for j in range(2):
            piece = slice(j * tile, (j + 1) * tile)
            for part in range(2):
                summed = acc[j, part * shots : (part + 1) * shots].astype(BF16).astype(F32)
                value = (summed + below[part, mine, piece].astype(F32)).astype(BF16)
                for send in sends:
                    send[part, :, piece] = value

    def next_up():
        zero = jnp.zeros((shots, tile), F32)
        for j in range(2):
            piece = slice(j * tile, (j + 1) * tile)
            halves = []
            for part in range(2):
                sums = here[part, :, piece].astype(F32)
                sums += jnp.where(meta[3] > 0, left[part, :, piece].astype(F32), zero)
                sums += jnp.where(meta[2] > 0, right[part, :, piece].astype(F32), zero)
                sums = sums.astype(BF16).astype(F32)
                value = (down_all[part, mine, piece].astype(F32) + sums).astype(BF16)
                up_all[part, mine, piece] = value
                halves.append(value)
            lhs[j] = stacked(*halves)

    def turn():
        for part in range(2):
            value = here[part]
            down_all[part, mine, :] = value
            up_all[part, mine, :] = value
        fill(0, here)

    def up():
        for j in range(6):
            acc[j] = jnp.zeros(acc.shape[1:], F32)

        def one(slot, carry):
            acc[meta[META + slots + slot]] += product(slot, meta[META + slot], 0)
            return carry

        lax.fori_loop(0, count, one, 0)
        for shift, send in zip((0, 1, -1), sends):
            for j in range(2):
                for part in range(2):
                    send[part, :, j * tile : (j + 1) * tile] = acc[
                        2 - 2 * shift + j, part * shots : (part + 1) * shots
                    ].astype(BF16)

    if has_halo:
        pl.when((mode == 1) & (layer == 0))(first)
    if any(at > 0 for _, at, _, _ in downs):
        pl.when((mode == 1) & (layer > 0))(next_down)
    if any(code == 3 for _, _, code, _ in ups):
        pl.when(mode == 3)(turn)
    if any(code in (2, 4) for _, _, code, _ in ups):
        pl.when((mode == 2) | (mode == 4))(next_up)
    if downs:
        pl.when(mode == 1)(down)
    if any(code in (2, 3) for _, _, code, _ in ups):
        pl.when((mode == 2) | (mode == 3))(up)


VMEM = pl.BlockSpec(memory_space=pltpu.VMEM)
SMEM = pl.BlockSpec(memory_space=pltpu.SMEM)


def run_step(waves, meta, tiles, here, left, right, below, down_all, up_all, halo):
    shots = here.shape[1]
    tile = tiles.shape[2]
    n_send = 3 if any(code != 1 for _, _, code, _ in waves) else 1
    return pl.pallas_call(
        functools.partial(step_kernel, waves, bool(halo)),
        out_shape=[pltpu.VMEM(here.shape, BF16)] * n_send + [pltpu.VMEM(down_all.shape, BF16)] * 2,
        in_specs=[SMEM] + [VMEM] * (7 + len(halo)),
        out_specs=[VMEM] * (n_send + 2),
        input_output_aliases={6: n_send, 7: n_send + 1},
        scratch_shapes=[
            pltpu.VMEM((6, 2 * shots, 2 * tile), BF16),
            pltpu.VMEM((6, 2 * shots, tile), F32),
        ],
        compiler_params=pltpu.CompilerParams(vmem_limit_bytes=24 << 20),
        name="step",
    )(meta, *map(resident, (tiles, here, left, right, below, down_all, up_all, *halo)))


def resident(x):
    return pltpu.with_memory_space_constraint(x, pltpu.VMEM)


def on_device(source, tile_data, tile_rows, tile_cols, tile_count):
    layers, ranges = lax.axis_size("layer"), lax.axis_size("blk")
    layer, rng = lax.axis_index("layer"), lax.axis_index("blk")
    own = source.shape[3] // tile_data.shape[3]
    first = rng * own
    meta = jnp.concatenate(
        [
            jnp.stack([layer, tile_count[0, 0], (rng > 0).astype(jnp.int32), (rng < ranges - 1).astype(jnp.int32)]),
            tile_rows[0] - first,
            tile_cols[0] - first + own,
        ]
    )
    sources = source[0]
    shots = source.shape[2] // WAVES

    def part(b):
        return lax.slice_in_dim(sources, b * shots, (b + 1) * shots, axis=1)

    def around(x, shift):
        return lax.ppermute(x, "blk", [(g, (g + shift) % ranges) for g in range(ranges)])

    halos = [(around(part(b), 1), around(part(b), -1)) for b in range(WAVES)]
    below = lax.ppermute(
        sources,
        AXES,
        [(((l + 1) % layers) * ranges + g, l * ranges + g) for l in range(layers) for g in range(ranges)],
    )
    tiles = tile_data[0]
    down_all, up_all = sources, jnp.zeros_like(sources)
    here = left = right = part(0)
    for waves in schedule(layers):
        halo = [h for b, at, code, _ in waves if code == 1 and at == 0 for h in halos[b]]
        *sends, down_all, up_all = run_step(
            waves, meta, tiles, here, left, right, below, down_all, up_all, halo
        )
        sends = dict(zip((0, 1, -1), sends * (3 // len(sends))))
        hops = sorted({hop for *_, hop in waves if hop is not None})
        if hops:
            got = {s: lax.ppermute(sends[s], AXES, route(hops, s, layers, ranges)) for s in ORDER}
            here, left, right = got[0], got[1], got[-1]
    return (down_all[None], up_all[None])


def solution(mesh):
    in_specs = (
        P("layer", None, None, "blk"),
        P("layer", "blk", None, None, None),
        P("layer", "blk"),
        P("layer", "blk"),
        P("layer", "blk"),
    )
    out_specs = (P("layer", None, None, "blk"), P("layer", None, None, "blk"))
    return jax.shard_map(
        on_device, mesh=mesh, in_specs=in_specs, out_specs=out_specs, check_vma=False
    )
```

```python
import functools

import jax
import jax.numpy as jnp
from jax import lax
from jax.experimental import pallas as pl
from jax.experimental.pallas import tpu as pltpu
from jax.sharding import PartitionSpec as P

WAVES = 2
PITCH = 4
ORDER = (0, 1, -1)
AXES = ("layer", "blk")
F32, BF16 = jnp.float32, jnp.bfloat16
META = 4


DOWN_RINGS = ((0, 1, 2, 3), (4, 5, 6, 7))
UP_RINGS = ((3, 2, 1, 0), (7, 6, 5, 4))
CROSS_DOWN = ((3, 4, 5, 6), (0, 1, 2, 7))
CROSS_UP = ((4, 3, 2, 1), (0, 7, 6, 5))
RINGS = {
    1: ((1, 2, 3, 4), (0, 7, 6, 5)),
    2: ((2, 3, 4, 5), (0, 1, 7, 6)),
    3: CROSS_DOWN,
    7: CROSS_DOWN,
    8: ((7, 6, 0, 1), (4, 5, 2, 3)),
    9: ((6, 5), (0, 1, 2, 3), (4, 7)),
    10: ((5, 4, 3, 2), (6, 7, 0, 1)),
    11: CROSS_UP,
    15: CROSS_UP,
}


def schedule(layers):
    top = layers - 1
    end = 2 * top + 1
    last = end + PITCH * (WAVES - 1)
    steps = []
    for step in range(last + 1):
        waves = []
        for b in range(WAVES):
            t = step - PITCH * b
            if 0 <= t <= end:
                code = 1 if t < top else 5 if t == top else 3 if t == top + 1 else 4 if t == end else 2
                waves.append((b, t if t <= top else end - t, code))
        rings = RINGS.get(step, DOWN_RINGS if step < top else UP_RINGS)
        steps.append((waves, rings if step < last else None))
    return steps


def route(rings, shift, ranges):
    pairs = []
    for ring in rings:
        for a, b in zip(ring, ring[1:] + ring[:1]):
            move = shift if abs(a - b) == 1 else 0
            pairs += [(a * ranges + g, b * ranges + (g + move) % ranges) for g in range(ranges)]
    return sorted(pairs)


def stacked(real, imag):
    return jnp.concatenate(
        [jnp.concatenate([real, imag], axis=0), jnp.concatenate([-imag, real], axis=0)], axis=1
    )


def sends_of(waves):
    return 3 if any(code in (2, 3) for _, _, code in waves) else 1


def step_kernel(waves, has_halo, meta, tiles, here, left, right, *rest):
    downs = [w for w in waves if w[2] == 1]
    ups = [w for w in waves if w[2] in (2, 3, 4)]
    n_below = max(1, len(downs))
    below, (down_in, up_in, *rest) = rest[:n_below], rest[n_below:]
    if has_halo:
        halo_l, halo_r, *rest = rest
    n_send = sends_of(waves)
    sends, (down_all, up_all, lhs, acc) = rest[:n_send], rest[n_send:]
    shots = here.shape[1]
    tile = tiles.shape[2]
    layer, count = meta[0], meta[1]
    slots = (meta.shape[0] - META) // 2
    mode, wave = jnp.int32(0), jnp.int32(0)
    for b, at, code in waves:
        mode = jnp.where(layer == at, code, mode)
        wave = jnp.where(layer == at, b, wave)
    mine = pl.ds(pl.multiple_of(wave * shots, shots), shots)

    def product(slot, source, contract):
        numbers = (((1,), (contract,)), ((), ()))
        x = lhs[source]
        return lax.dot_general(x[:, :tile], tiles[slot, 0], numbers, preferred_element_type=F32) + (
            lax.dot_general(x[:, tile:], tiles[slot, 1], numbers, preferred_element_type=F32)
        )

    def fill(index, ref, rows=slice(None)):
        for j in range(2):
            piece = slice(j * tile, (j + 1) * tile)
            lhs[index + j] = stacked(ref[0, rows, piece], ref[1, rows, piece])

    def next_down():
        fill(0, left)
        fill(2, here)
        fill(4, right)
        down_all[0, mine, :] = here[0]
        down_all[1, mine, :] = here[1]

    def first():
        fill(0, halo_l)
        fill(2, down_all, mine)
        fill(4, halo_r)

    def down():
        for j in range(2):
            acc[j] = jnp.zeros(acc.shape[1:], F32)

        def one(slot, carry):
            acc[meta[META + slot]] += product(slot, meta[META + slots + slot], 1)
            return carry

        lax.fori_loop(0, count, one, 0)
        for j in range(2):
            piece = slice(j * tile, (j + 1) * tile)
            for part in range(2):
                summed = acc[j, part * shots : (part + 1) * shots].astype(BF16).astype(F32)
                added = below[0][part, :, piece].astype(F32)
                for (b, _, _), more in zip(downs[1:], below[1:]):
                    added = jnp.where(wave == b, more[part, :, piece].astype(F32), added)
                value = (summed + added).astype(BF16)
                for send in sends:
                    send[part, :, piece] = value

    def next_up():
        zero = jnp.zeros((shots, tile), F32)
        for j in range(2):
            piece = slice(j * tile, (j + 1) * tile)
            halves = []
            for part in range(2):
                sums = here[part, :, piece].astype(F32)
                sums += jnp.where(meta[2] > 0, left[part, :, piece].astype(F32), zero)
                sums += jnp.where(meta[3] > 0, right[part, :, piece].astype(F32), zero)
                sums = sums.astype(BF16).astype(F32)
                value = (down_all[part, mine, piece].astype(F32) + sums).astype(BF16)
                up_all[part, mine, piece] = value
                halves.append(value)
            lhs[j] = stacked(*halves)

    def keep():
        for part in range(2):
            down_all[part, mine, :] = here[part]

    def turn():
        for part in range(2):
            up_all[part, mine, :] = down_all[part, mine, :]
        fill(0, down_all, mine)

    def up():
        for j in range(6):
            acc[j] = jnp.zeros(acc.shape[1:], F32)

        def one(slot, carry):
            acc[meta[META + slots + slot]] += product(slot, meta[META + slot], 0)
            return carry

        lax.fori_loop(0, count, one, 0)
        for shift, send in zip((0, 1, -1), sends):
            for j in range(2):
                for part in range(2):
                    send[part, :, j * tile : (j + 1) * tile] = acc[
                        2 + 2 * shift + j, part * shots : (part + 1) * shots
                    ].astype(BF16)

    if has_halo:
        pl.when((mode == 1) & (layer == 0))(first)
    if any(at > 0 for _, at, _ in downs):
        pl.when((mode == 1) & (layer > 0))(next_down)
    if any(code == 5 for _, _, code in waves):
        pl.when(mode == 5)(keep)
    if any(code == 3 for _, _, code in ups):
        pl.when(mode == 3)(turn)
    if any(code in (2, 4) for _, _, code in ups):
        pl.when((mode == 2) | (mode == 4))(next_up)
    if downs:
        pl.when(mode == 1)(down)
    if any(code in (2, 3) for _, _, code in ups):
        pl.when((mode == 2) | (mode == 3))(up)


VMEM = pl.BlockSpec(memory_space=pltpu.VMEM)
SMEM = pl.BlockSpec(memory_space=pltpu.SMEM)


def run_step(waves, meta, tiles, here, left, right, below, down_all, up_all, halo):
    shots = here.shape[1]
    tile = tiles.shape[2]
    n_send = sends_of(waves)
    at = 5 + len(below)
    return pl.pallas_call(
        functools.partial(step_kernel, waves, bool(halo)),
        out_shape=[pltpu.VMEM(here.shape, BF16)] * n_send + [pltpu.VMEM(down_all.shape, BF16)] * 2,
        in_specs=[SMEM] + [VMEM] * (6 + len(below) + len(halo)),
        out_specs=[VMEM] * (n_send + 2),
        input_output_aliases={at: n_send, at + 1: n_send + 1},
        scratch_shapes=[
            pltpu.VMEM((6, 2 * shots, 2 * tile), BF16),
            pltpu.VMEM((6, 2 * shots, tile), F32),
        ],
        compiler_params=pltpu.CompilerParams(vmem_limit_bytes=24 << 20),
        name="step",
    )(meta, *map(resident, (tiles, here, left, right, *below, down_all, up_all, *halo)))


def resident(x):
    return pltpu.with_memory_space_constraint(x, pltpu.VMEM)


def on_device(source, tile_data, tile_rows, tile_cols, tile_count):
    layers, ranges = lax.axis_size("layer"), lax.axis_size("blk")
    layer, rng = lax.axis_index("layer"), lax.axis_index("blk")
    own = source.shape[3] // tile_data.shape[3]
    first = rng * own
    meta = jnp.concatenate(
        [
            jnp.stack([layer, tile_count[0, 0], (rng > 0).astype(jnp.int32), (rng < ranges - 1).astype(jnp.int32)]),
            tile_rows[0] - first,
            tile_cols[0] - first + own,
        ]
    )
    sources = source[0]
    shots = source.shape[2] // WAVES

    def part(b):
        return lax.slice_in_dim(sources, b * shots, (b + 1) * shots, axis=1)

    def around(x, shift):
        pairs = [(g, (g + shift) % ranges) for g in range(ranges)]
        pairs += [
            (l * ranges + g, (l % (layers - 1) + 1) * ranges + g)
            for l in range(1, layers)
            for g in range(ranges)
        ]
        return lax.ppermute(x, AXES, pairs)

    def back(x):
        pairs = [(l * ranges + g, (l - 1) % layers * ranges + g) for l in range(layers) for g in range(ranges)]
        return lax.ppermute(x, AXES, pairs)

    halos = [(around(part(b), 1), around(part(b), -1)) for b in range(WAVES)]
    belows = [back(part(b)) for b in range(WAVES)]
    tiles = tile_data[0]
    down_all, up_all = sources, jnp.zeros_like(sources)
    here = left = right = part(0)
    for waves, rings in schedule(layers):
        halo = [h for b, at, code in waves if code == 1 and at == 0 for h in halos[b]]
        below = [belows[b] for b, _, code in waves if code == 1] or belows[:1]
        *sends, down_all, up_all = run_step(
            waves, meta, tiles, here, left, right, below, down_all, up_all, halo
        )
        if rings:
            sends = dict(zip((0, 1, -1), sends * (3 // len(sends))))
            got = {s: lax.ppermute(sends[s], AXES, route(rings, s, ranges)) for s in ORDER}
            here, left, right = got[0], got[1], got[-1]
    return (down_all[None], up_all[None])


def solution(mesh):
    in_specs = (
        P("layer", None, None, "blk"),
        P("layer", "blk", None, None, None),
        P("layer", "blk"),
        P("layer", "blk"),
        P("layer", "blk"),
    )
    out_specs = (P("layer", None, None, "blk"), P("layer", None, None, "blk"))
    return jax.shard_map(
        on_device, mesh=mesh, in_specs=in_specs, out_specs=out_specs, check_vma=False
    )
```

```python
import functools

import jax
import jax.numpy as jnp
from jax import lax
from jax.experimental import pallas as pl
from jax.experimental.pallas import tpu as pltpu
from jax.sharding import PartitionSpec as P

WAVES = 2
PITCH = 2
ORDER = (0, 1, -1)
AXES = ("layer", "blk")
F32, BF16 = jnp.float32, jnp.bfloat16
META = 4


def links(sends, odd, layers):
    pairs = [(k, (k + 1) % layers) for k in range(odd, layers, 2)]
    ways = {(a, b) for a, b in sends}
    if len({a < b for a, b in sends}) == 2:
        (hop,) = {min(way) for way in sends}
        plus = ways
        minus = {(hop - 2, hop - 1), (hop - 1, hop - 2)}
    else:
        (down,) = {a < b for a, b in sends}
        most = max(min(way) for way in sends)
        hops = {most, most - 2 if most > 1 else most + 2}
        way = {k: (k, m) if down else (m, k) for k, m in pairs}
        plus = {way[k] for k in hops}
        minus = {way[k] for k, _ in pairs if k not in hops}
    share = {**dict.fromkeys(plus, 1), **dict.fromkeys(minus, -1)}
    return tuple((a, b, share.get((a, b), 0)) for k, m in pairs for a, b in ((k, m), (m, k)))


def route(edges, shift, ranges):
    to, free_to, free_from = {}, {}, {}
    for a, b, share in edges:
        for g in range(ranges):
            if 0 <= g + share * shift < ranges:
                to[a * ranges + g] = b * ranges + g + share * shift
    taken = set(to.values())
    for g in range(ranges):
        sources = [a * ranges + g for a, _, _ in edges if a * ranges + g not in to]
        targets = [b * ranges + g for _, b, _ in edges if b * ranges + g not in taken]
        to.update(zip(sources, targets, strict=True))
    return sorted(to.items())


def schedule(layers):
    top = layers - 1
    end = 2 * top + 1
    steps = []
    for step in range(end + 1 + PITCH * (WAVES - 1)):
        waves, sends = [], []
        for b in range(WAVES):
            t = step - PITCH * b
            if 0 <= t < top:
                waves.append((b, t, 1))
                sends.append((t, t + 1))
            elif t == top:
                waves.append((b, top, 5))
            elif top < t < end:
                waves.append((b, end - t, 3 if t == top + 1 else 2))
                sends.append((end - t, end - t - 1))
            elif t == end:
                waves.append((b, 0, 4))
        steps.append((waves, links(sends, step % 2, layers) if sends else None))
    return steps


def stacked(real, imag):
    return jnp.concatenate(
        [jnp.concatenate([real, imag], axis=0), jnp.concatenate([-imag, real], axis=0)], axis=1
    )


def sends_of(waves):
    return 3 if any(code in (2, 3) for _, _, code in waves) else 1


def step_kernel(waves, has_halo, meta, tiles, here, left, right, *rest):
    downs = [w for w in waves if w[2] == 1]
    ups = [w for w in waves if w[2] in (2, 3, 4)]
    n_below = max(1, len(downs))
    below, (down_in, up_in, *rest) = rest[:n_below], rest[n_below:]
    if has_halo:
        halo_l, halo_r, *rest = rest
    n_send = sends_of(waves)
    sends, (down_all, up_all, lhs, acc) = rest[:n_send], rest[n_send:]
    shots = here.shape[1]
    tile = tiles.shape[2]
    layer, count = meta[0], meta[1]
    slots = (meta.shape[0] - META) // 2
    mode, wave = jnp.int32(0), jnp.int32(0)
    for b, at, code in waves:
        mode = jnp.where(layer == at, code, mode)
        wave = jnp.where(layer == at, b, wave)
    mine = pl.ds(pl.multiple_of(wave * shots, shots), shots)

    def product(slot, source, contract):
        numbers = (((1,), (contract,)), ((), ()))
        x = lhs[source]
        return lax.dot_general(x[:, :tile], tiles[slot, 0], numbers, preferred_element_type=F32) + (
            lax.dot_general(x[:, tile:], tiles[slot, 1], numbers, preferred_element_type=F32)
        )

    def fill(index, ref, rows=slice(None)):
        for j in range(2):
            piece = slice(j * tile, (j + 1) * tile)
            lhs[index + j] = stacked(ref[0, rows, piece], ref[1, rows, piece])

    def next_down():
        fill(0, left)
        fill(2, here)
        fill(4, right)
        down_all[0, mine, :] = here[0]
        down_all[1, mine, :] = here[1]

    def first():
        fill(0, halo_l)
        fill(2, down_all, mine)
        fill(4, halo_r)

    def down():
        for j in range(2):
            acc[j] = jnp.zeros(acc.shape[1:], F32)

        def one(slot, carry):
            acc[meta[META + slot]] += product(slot, meta[META + slots + slot], 1)
            return carry

        lax.fori_loop(0, count, one, 0)
        for j in range(2):
            piece = slice(j * tile, (j + 1) * tile)
            for part in range(2):
                summed = acc[j, part * shots : (part + 1) * shots].astype(BF16).astype(F32)
                added = below[0][part, :, piece].astype(F32)
                for (b, _, _), more in zip(downs[1:], below[1:]):
                    added = jnp.where(wave == b, more[part, :, piece].astype(F32), added)
                value = (summed + added).astype(BF16)
                for send in sends:
                    send[part, :, piece] = value

    def next_up():
        zero = jnp.zeros((shots, tile), F32)
        for j in range(2):
            piece = slice(j * tile, (j + 1) * tile)
            halves = []
            for part in range(2):
                sums = here[part, :, piece].astype(F32)
                sums += jnp.where(meta[2] > 0, left[part, :, piece].astype(F32), zero)
                sums += jnp.where(meta[3] > 0, right[part, :, piece].astype(F32), zero)
                sums = sums.astype(BF16).astype(F32)
                value = (down_all[part, mine, piece].astype(F32) + sums).astype(BF16)
                up_all[part, mine, piece] = value
                halves.append(value)
            lhs[j] = stacked(*halves)

    def keep():
        for part in range(2):
            down_all[part, mine, :] = here[part]

    def turn():
        for part in range(2):
            up_all[part, mine, :] = down_all[part, mine, :]
        fill(0, down_all, mine)

    def up():
        for j in range(6):
            acc[j] = jnp.zeros(acc.shape[1:], F32)

        def one(slot, carry):
            acc[meta[META + slots + slot]] += product(slot, meta[META + slot], 0)
            return carry

        lax.fori_loop(0, count, one, 0)
        for shift, send in zip((0, 1, -1), sends):
            for j in range(2):
                for part in range(2):
                    send[part, :, j * tile : (j + 1) * tile] = acc[
                        2 + 2 * shift + j, part * shots : (part + 1) * shots
                    ].astype(BF16)

    if has_halo:
        pl.when((mode == 1) & (layer == 0))(first)
    if any(at > 0 for _, at, _ in downs):
        pl.when((mode == 1) & (layer > 0))(next_down)
    if any(code == 5 for _, _, code in waves):
        pl.when(mode == 5)(keep)
    if any(code == 3 for _, _, code in ups):
        pl.when(mode == 3)(turn)
    if any(code in (2, 4) for _, _, code in ups):
        pl.when((mode == 2) | (mode == 4))(next_up)
    if downs:
        pl.when(mode == 1)(down)
    if any(code in (2, 3) for _, _, code in ups):
        pl.when((mode == 2) | (mode == 3))(up)


VMEM = pl.BlockSpec(memory_space=pltpu.VMEM)
SMEM = pl.BlockSpec(memory_space=pltpu.SMEM)


def run_step(waves, meta, tiles, here, left, right, below, down_all, up_all, halo):
    shots = here.shape[1]
    tile = tiles.shape[2]
    n_send = sends_of(waves)
    at = 5 + len(below)
    return pl.pallas_call(
        functools.partial(step_kernel, waves, bool(halo)),
        out_shape=[pltpu.VMEM(here.shape, BF16)] * n_send + [pltpu.VMEM(down_all.shape, BF16)] * 2,
        in_specs=[SMEM] + [VMEM] * (6 + len(below) + len(halo)),
        out_specs=[VMEM] * (n_send + 2),
        input_output_aliases={at: n_send, at + 1: n_send + 1},
        scratch_shapes=[
            pltpu.VMEM((6, 2 * shots, 2 * tile), BF16),
            pltpu.VMEM((6, 2 * shots, tile), F32),
        ],
        compiler_params=pltpu.CompilerParams(vmem_limit_bytes=24 << 20),
        name="step",
    )(meta, *map(resident, (tiles, here, left, right, *below, down_all, up_all, *halo)))


def resident(x):
    return pltpu.with_memory_space_constraint(x, pltpu.VMEM)


def on_device(source, tile_data, tile_rows, tile_cols, tile_count):
    layers, ranges = lax.axis_size("layer"), lax.axis_size("blk")
    layer, rng = lax.axis_index("layer"), lax.axis_index("blk")
    own = source.shape[3] // tile_data.shape[3]
    first = rng * own
    meta = jnp.concatenate(
        [
            jnp.stack([layer, tile_count[0, 0], (rng > 0).astype(jnp.int32), (rng < ranges - 1).astype(jnp.int32)]),
            tile_rows[0] - first,
            tile_cols[0] - first + own,
        ]
    )
    sources = source[0]
    shots = source.shape[2] // WAVES

    def part(b):
        return lax.slice_in_dim(sources, b * shots, (b + 1) * shots, axis=1)

    def around(x, shift):
        edges = [(0, 0, 1), (2, 2, -1), (1, 3, 0), (3, 1, 0)]
        edges += [(l, l ^ 1, 0) for l in range(4, layers)]
        return lax.ppermute(x, AXES, route(edges, shift, ranges))

    def back(x):
        pairs = [(l * ranges + g, (l - 1) % layers * ranges + g) for l in range(layers) for g in range(ranges)]
        return lax.ppermute(x, AXES, pairs)

    halos = [(around(part(b), 1), around(part(b), -1)) for b in range(WAVES)]
    belows = [back(part(b)) for b in range(WAVES)]
    tiles = tile_data[0]
    down_all, up_all = sources, jnp.zeros_like(sources)
    here = left = right = part(0)
    for waves, edges in schedule(layers):
        halo = [h for b, at, code in waves if code == 1 and at == 0 for h in halos[b]]
        below = [belows[b] for b, _, code in waves if code == 1] or belows[:1]
        *sends, down_all, up_all = run_step(
            waves, meta, tiles, here, left, right, below, down_all, up_all, halo
        )
        if edges:
            sends = dict(zip((0, 1, -1), sends * (3 // len(sends))))
            got = {s: lax.ppermute(sends[s], AXES, route(edges, s, ranges)) for s in ORDER}
            here, left, right = got[0], got[1], got[-1]
    return (down_all[None], up_all[None])


def solution(mesh):
    in_specs = (
        P("layer", None, None, "blk"),
        P("layer", "blk", None, None, None),
        P("layer", "blk"),
        P("layer", "blk"),
        P("layer", "blk"),
    )
    out_specs = (P("layer", None, None, "blk"), P("layer", None, None, "blk"))
    return jax.shard_map(
        on_device, mesh=mesh, in_specs=in_specs, out_specs=out_specs, check_vma=False
    )
```

```python
import functools

import jax
import jax.numpy as jnp
from jax import lax
from jax.experimental import pallas as pl
from jax.experimental.pallas import tpu as pltpu
from jax.sharding import PartitionSpec as P

WAVES = 2
PITCH = 2
ORDER = (0, 1, -1)
AXES = ("layer", "blk")
F32, BF16 = jnp.float32, jnp.bfloat16
META = 4


def links(sends, odd, layers):
    pairs = [(k, (k + 1) % layers) for k in range(odd, layers, 2)]
    ways = {(a, b) for a, b in sends}
    if len({a < b for a, b in sends}) == 2:
        (hop,) = {min(way) for way in sends}
        plus = ways
        minus = {(hop - 2, hop - 1), (hop - 1, hop - 2)}
    else:
        (down,) = {a < b for a, b in sends}
        most = max(min(way) for way in sends)
        hops = {most, most - 2 if most > 1 else most + 2}
        way = {k: (k, m) if down else (m, k) for k, m in pairs}
        plus = {way[k] for k in hops}
        minus = {way[k] for k, _ in pairs if k not in hops}
    share = {**dict.fromkeys(plus, 1), **dict.fromkeys(minus, -1)}
    return tuple((a, b, share.get((a, b), 0)) for k, m in pairs for a, b in ((k, m), (m, k)))


def route(edges, shift, ranges):
    to, free_to, free_from = {}, {}, {}
    for a, b, share in edges:
        for g in range(ranges):
            if 0 <= g + share * shift < ranges:
                to[a * ranges + g] = b * ranges + g + share * shift
    taken = set(to.values())
    for g in range(ranges):
        sources = [a * ranges + g for a, _, _ in edges if a * ranges + g not in to]
        targets = [b * ranges + g for _, b, _ in edges if b * ranges + g not in taken]
        to.update(zip(sources, targets, strict=True))
    return sorted(to.items())


def schedule(layers):
    top = layers - 1
    end = 2 * top + 1
    steps = []
    for step in range(end + 1 + PITCH * (WAVES - 1)):
        waves, sends = [], []
        for b in range(WAVES):
            t = step - PITCH * b
            if 0 <= t < top:
                waves.append((b, t, 1))
                sends.append((t, t + 1))
            elif t == top:
                waves.append((b, top, 5))
            elif top < t < end:
                waves.append((b, end - t, 3 if t == top + 1 else 2))
                sends.append((end - t, end - t - 1))
            elif t == end:
                waves.append((b, 0, 4))
        steps.append((waves, links(sends, step % 2, layers) if sends else None))
    return steps


def stacked(real, imag):
    return jnp.concatenate(
        [jnp.concatenate([real, imag], axis=0), jnp.concatenate([-imag, real], axis=0)], axis=1
    )


def sends_of(waves):
    return 3 if any(code in (2, 3) for _, _, code in waves) else 1


def step_kernel(waves, has_halo, meta, here, left, right, *rest):
    downs = [w for w in waves if w[2] == 1]
    ups = [w for w in waves if w[2] in (2, 3, 4)]
    turned, *rest = rest if downs else (None, *rest)
    tiles, *rest = rest if ups else (None, *rest)
    n_below = max(1, len(downs))
    below, (down_in, up_in, *rest) = rest[:n_below], rest[n_below:]
    if has_halo:
        halo_l, halo_r, *rest = rest
    n_send = sends_of(waves)
    sends, (down_all, up_all, lhs, acc) = rest[:n_send], rest[n_send:]
    shots = here.shape[1]
    tile = here.shape[2] // 2
    layer, count = meta[0], meta[1]
    slots = (meta.shape[0] - META) // 2
    mode, wave = jnp.int32(0), jnp.int32(0)
    for b, at, code in waves:
        mode = jnp.where(layer == at, code, mode)
        wave = jnp.where(layer == at, b, wave)
    mine = pl.ds(pl.multiple_of(wave * shots, shots), shots)

    def product(tiles, slot, source):
        numbers = (((1,), (0,)), ((), ()))
        x = lhs[source]
        return lax.dot_general(x[:, :tile], tiles[slot, 0], numbers, preferred_element_type=F32) + (
            lax.dot_general(x[:, tile:], tiles[slot, 1], numbers, preferred_element_type=F32)
        )

    def fill(index, ref, rows=slice(None)):
        for j in range(2):
            piece = slice(j * tile, (j + 1) * tile)
            lhs[index + j] = stacked(ref[0, rows, piece], ref[1, rows, piece])

    def next_down():
        fill(0, left)
        fill(2, here)
        fill(4, right)
        down_all[0, mine, :] = here[0]
        down_all[1, mine, :] = here[1]

    def first():
        fill(0, halo_l)
        fill(2, down_all, mine)
        fill(4, halo_r)

    def down():
        for j in range(2):
            acc[j] = jnp.zeros(acc.shape[1:], F32)

        def one(slot, carry):
            acc[meta[META + slot]] += product(turned, slot, meta[META + slots + slot])
            return carry

        lax.fori_loop(0, count, one, 0)
        for j in range(2):
            piece = slice(j * tile, (j + 1) * tile)
            for part in range(2):
                summed = acc[j, part * shots : (part + 1) * shots].astype(BF16).astype(F32)
                added = below[0][part, :, piece].astype(F32)
                for (b, _, _), more in zip(downs[1:], below[1:]):
                    added = jnp.where(wave == b, more[part, :, piece].astype(F32), added)
                value = (summed + added).astype(BF16)
                for send in sends:
                    send[part, :, piece] = value

    def next_up():
        zero = jnp.zeros((shots, tile), F32)
        for j in range(2):
            piece = slice(j * tile, (j + 1) * tile)
            halves = []
            for part in range(2):
                sums = here[part, :, piece].astype(F32)
                sums += jnp.where(meta[2] > 0, left[part, :, piece].astype(F32), zero)
                sums += jnp.where(meta[3] > 0, right[part, :, piece].astype(F32), zero)
                sums = sums.astype(BF16).astype(F32)
                value = (down_all[part, mine, piece].astype(F32) + sums).astype(BF16)
                up_all[part, mine, piece] = value
                halves.append(value)
            lhs[j] = stacked(*halves)

    def keep():
        for part in range(2):
            down_all[part, mine, :] = here[part]

    def turn():
        for part in range(2):
            up_all[part, mine, :] = down_all[part, mine, :]
        fill(0, down_all, mine)

    def up():
        for j in range(6):
            acc[j] = jnp.zeros(acc.shape[1:], F32)

        def one(slot, carry):
            acc[meta[META + slots + slot]] += product(tiles, slot, meta[META + slot])
            return carry

        lax.fori_loop(0, count, one, 0)
        for shift, send in zip((0, 1, -1), sends):
            for j in range(2):
                for part in range(2):
                    send[part, :, j * tile : (j + 1) * tile] = acc[
                        2 + 2 * shift + j, part * shots : (part + 1) * shots
                    ].astype(BF16)

    if has_halo:
        pl.when((mode == 1) & (layer == 0))(first)
    if any(at > 0 for _, at, _ in downs):
        pl.when((mode == 1) & (layer > 0))(next_down)
    if any(code == 5 for _, _, code in waves):
        pl.when(mode == 5)(keep)
    if any(code == 3 for _, _, code in ups):
        pl.when(mode == 3)(turn)
    if any(code in (2, 4) for _, _, code in ups):
        pl.when((mode == 2) | (mode == 4))(next_up)
    if downs:
        pl.when(mode == 1)(down)
    if any(code in (2, 3) for _, _, code in ups):
        pl.when((mode == 2) | (mode == 3))(up)


VMEM = pl.BlockSpec(memory_space=pltpu.VMEM)
SMEM = pl.BlockSpec(memory_space=pltpu.SMEM)


def run_step(waves, meta, turned, tiles, here, left, right, below, down_all, up_all, halo):
    shots = here.shape[1]
    tile = here.shape[2] // 2
    codes = {code for _, _, code in waves}
    used = ([turned] if 1 in codes else []) + ([tiles] if codes & {2, 3, 4} else [])
    n_send = sends_of(waves)
    at = 4 + len(used) + len(below)
    return pl.pallas_call(
        functools.partial(step_kernel, waves, bool(halo)),
        out_shape=[pltpu.VMEM(here.shape, BF16)] * n_send + [pltpu.VMEM(down_all.shape, BF16)] * 2,
        in_specs=[SMEM] + [VMEM] * (5 + len(used) + len(below) + len(halo)),
        out_specs=[VMEM] * (n_send + 2),
        input_output_aliases={at: n_send, at + 1: n_send + 1},
        scratch_shapes=[
            pltpu.VMEM((6, 2 * shots, 2 * tile), BF16),
            pltpu.VMEM((6, 2 * shots, tile), F32),
        ],
        compiler_params=pltpu.CompilerParams(vmem_limit_bytes=24 << 20),
        name="step",
    )(meta, *map(resident, (here, left, right, *used, *below, down_all, up_all, *halo)))


def resident(x):
    return pltpu.with_memory_space_constraint(x, pltpu.VMEM)


def on_device(source, tile_data, tile_rows, tile_cols, tile_count):
    layers, ranges = lax.axis_size("layer"), lax.axis_size("blk")
    layer, rng = lax.axis_index("layer"), lax.axis_index("blk")
    own = source.shape[3] // tile_data.shape[3]
    first = rng * own
    meta = jnp.concatenate(
        [
            jnp.stack([layer, tile_count[0, 0], (rng > 0).astype(jnp.int32), (rng < ranges - 1).astype(jnp.int32)]),
            tile_rows[0] - first,
            tile_cols[0] - first + own,
        ]
    )
    sources = source[0]
    shots = source.shape[2] // WAVES

    def part(b):
        return lax.slice_in_dim(sources, b * shots, (b + 1) * shots, axis=1)

    def around(x, shift):
        edges = [(0, 0, 1), (2, 2, -1), (1, 3, 0), (3, 1, 0)]
        edges += [(l, l ^ 1, 0) for l in range(4, layers)]
        return lax.ppermute(x, AXES, route(edges, shift, ranges))

    def back(x):
        pairs = [(l * ranges + g, (l - 1) % layers * ranges + g) for l in range(layers) for g in range(ranges)]
        return lax.ppermute(x, AXES, pairs)

    halos = [(around(part(b), 1), around(part(b), -1)) for b in range(WAVES)]
    belows = [back(part(b)) for b in range(WAVES)]
    tiles = tile_data[0]
    turned = jnp.swapaxes(tiles, 2, 3)
    down_all, up_all = sources, jnp.zeros_like(sources)
    here = left = right = part(0)
    for waves, edges in schedule(layers):
        halo = [h for b, at, code in waves if code == 1 and at == 0 for h in halos[b]]
        below = [belows[b] for b, _, code in waves if code == 1] or belows[:1]
        *sends, down_all, up_all = run_step(
            waves, meta, turned, tiles, here, left, right, below, down_all, up_all, halo
        )
        if edges:
            sends = dict(zip((0, 1, -1), sends * (3 // len(sends))))
            got = {s: lax.ppermute(sends[s], AXES, route(edges, s, ranges)) for s in ORDER}
            here, left, right = got[0], got[1], got[-1]
    return (down_all[None], up_all[None])


def solution(mesh):
    in_specs = (
        P("layer", None, None, "blk"),
        P("layer", "blk", None, None, None),
        P("layer", "blk"),
        P("layer", "blk"),
        P("layer", "blk"),
    )
    out_specs = (P("layer", None, None, "blk"), P("layer", None, None, "blk"))
    return jax.shard_map(
        on_device, mesh=mesh, in_specs=in_specs, out_specs=out_specs, check_vma=False
    )
```

```python
import functools

import jax
import jax.numpy as jnp
from jax import lax
from jax.experimental import pallas as pl
from jax.experimental.pallas import tpu as pltpu
from jax.sharding import PartitionSpec as P

WAVES = 2
PITCH = 2
ORDER = (0, 1, -1)
AXES = ("layer", "blk")
F32, BF16 = jnp.float32, jnp.bfloat16
META = 4


def links(sends, odd, layers):
    pairs = [(k, (k + 1) % layers) for k in range(odd, layers, 2)]
    ways = {(a, b) for a, b in sends}
    if len({a < b for a, b in sends}) == 2:
        (hop,) = {min(way) for way in sends}
        plus = ways
        minus = {(hop - 2, hop - 1), (hop - 1, hop - 2)}
    else:
        (down,) = {a < b for a, b in sends}
        most = max(min(way) for way in sends)
        hops = {most, most - 2 if most > 1 else most + 2}
        way = {k: (k, m) if down else (m, k) for k, m in pairs}
        plus = {way[k] for k in hops}
        minus = {way[k] for k, _ in pairs if k not in hops}
    share = {**dict.fromkeys(plus, 1), **dict.fromkeys(minus, -1)}
    return tuple((a, b, share.get((a, b), 0)) for k, m in pairs for a, b in ((k, m), (m, k)))


def route(edges, shift, ranges):
    to, free_to, free_from = {}, {}, {}
    for a, b, share in edges:
        for g in range(ranges):
            if 0 <= g + share * shift < ranges:
                to[a * ranges + g] = b * ranges + g + share * shift
    taken = set(to.values())
    for g in range(ranges):
        sources = [a * ranges + g for a, _, _ in edges if a * ranges + g not in to]
        targets = [b * ranges + g for _, b, _ in edges if b * ranges + g not in taken]
        to.update(zip(sources, targets, strict=True))
    return sorted(to.items())


def schedule(layers):
    top = layers - 1
    end = 2 * top + 1
    steps = []
    for step in range(end + 1 + PITCH * (WAVES - 1)):
        waves, sends = [], []
        for b in range(WAVES):
            t = step - PITCH * b
            if 0 <= t < top:
                waves.append((b, t, 1))
                sends.append((t, t + 1))
            elif t == top:
                waves.append((b, top, 5))
            elif top < t < end:
                waves.append((b, end - t, 3 if t == top + 1 else 2))
                sends.append((end - t, end - t - 1))
            elif t == end:
                waves.append((b, 0, 4))
        steps.append((waves, links(sends, step % 2, layers) if sends else None))
    return steps


def stacked(real, imag):
    return jnp.concatenate(
        [jnp.concatenate([real, imag], axis=0), jnp.concatenate([-imag, real], axis=0)], axis=1
    )


def sends_of(waves):
    return 3 if any(code in (2, 3) for _, _, code in waves) else 1


def writes_down(waves):
    return any(code in (1, 5) for _, _, code in waves)


def step_kernel(waves, has_halo, meta, here, left, right, *rest):
    downs = [w for w in waves if w[2] == 1]
    ups = [w for w in waves if w[2] in (2, 3, 4)]
    turned, *rest = rest if downs else (None, *rest)
    tiles, *rest = rest if ups else (None, *rest)
    n_below = max(1, len(downs))
    below, (down_in, up_in, *rest) = rest[:n_below], rest[n_below:]
    if has_halo:
        halo_l, halo_r, *rest = rest
    n_send = sends_of(waves)
    sends, rest = rest[:n_send], rest[n_send:]
    down_all, *rest = rest if writes_down(waves) else (down_in, *rest)
    up_all, lhs, acc = rest
    shots = here.shape[1]
    tile = here.shape[2] // 2
    layer, count = meta[0], meta[1]
    slots = (meta.shape[0] - META) // 2
    mode, wave = jnp.int32(0), jnp.int32(0)
    for b, at, code in waves:
        mode = jnp.where(layer == at, code, mode)
        wave = jnp.where(layer == at, b, wave)
    mine = pl.ds(pl.multiple_of(wave * shots, shots), shots)

    def product(tiles, slot, source):
        numbers = (((1,), (0,)), ((), ()))
        x = lhs[source]
        return lax.dot_general(x[:, :tile], tiles[slot, 0], numbers, preferred_element_type=F32) + (
            lax.dot_general(x[:, tile:], tiles[slot, 1], numbers, preferred_element_type=F32)
        )

    def fill(index, ref, rows=slice(None)):
        for j in range(2):
            piece = slice(j * tile, (j + 1) * tile)
            lhs[index + j] = stacked(ref[0, rows, piece], ref[1, rows, piece])

    def next_down():
        fill(0, left)
        fill(2, here)
        fill(4, right)
        down_all[0, mine, :] = here[0]
        down_all[1, mine, :] = here[1]

    def first():
        fill(0, halo_l)
        fill(2, down_all, mine)
        fill(4, halo_r)

    def down():
        for j in range(2):
            acc[j] = jnp.zeros(acc.shape[1:], F32)

        def one(slot, carry):
            acc[meta[META + slot]] += product(turned, slot, meta[META + slots + slot])
            return carry

        lax.fori_loop(0, count, one, 0)
        for j in range(2):
            piece = slice(j * tile, (j + 1) * tile)
            for part in range(2):
                summed = acc[j, part * shots : (part + 1) * shots].astype(BF16).astype(F32)
                added = below[0][part, :, piece].astype(F32)
                for (b, _, _), more in zip(downs[1:], below[1:]):
                    added = jnp.where(wave == b, more[part, :, piece].astype(F32), added)
                value = (summed + added).astype(BF16)
                for send in sends:
                    send[part, :, piece] = value

    def next_up():
        zero = jnp.zeros((shots, tile), F32)
        for j in range(2):
            piece = slice(j * tile, (j + 1) * tile)
            halves = []
            for part in range(2):
                sums = here[part, :, piece].astype(F32)
                sums += jnp.where(meta[2] > 0, left[part, :, piece].astype(F32), zero)
                sums += jnp.where(meta[3] > 0, right[part, :, piece].astype(F32), zero)
                sums = sums.astype(BF16).astype(F32)
                value = (down_all[part, mine, piece].astype(F32) + sums).astype(BF16)
                up_all[part, mine, piece] = value
                halves.append(value)
            lhs[j] = stacked(*halves)

    def keep():
        for part in range(2):
            down_all[part, mine, :] = here[part]

    def turn():
        for part in range(2):
            up_all[part, mine, :] = down_all[part, mine, :]
        fill(0, down_all, mine)

    def up():
        for j in range(6):
            acc[j] = jnp.zeros(acc.shape[1:], F32)

        def one(slot, carry):
            acc[meta[META + slots + slot]] += product(tiles, slot, meta[META + slot])
            return carry

        lax.fori_loop(0, count, one, 0)
        for shift, send in zip((0, 1, -1), sends):
            for j in range(2):
                for part in range(2):
                    send[part, :, j * tile : (j + 1) * tile] = acc[
                        2 + 2 * shift + j, part * shots : (part + 1) * shots
                    ].astype(BF16)

    if has_halo:
        pl.when((mode == 1) & (layer == 0))(first)
    if any(at > 0 for _, at, _ in downs):
        pl.when((mode == 1) & (layer > 0))(next_down)
    if any(code == 5 for _, _, code in waves):
        pl.when(mode == 5)(keep)
    if any(code == 3 for _, _, code in ups):
        pl.when(mode == 3)(turn)
    if any(code in (2, 4) for _, _, code in ups):
        pl.when((mode == 2) | (mode == 4))(next_up)
    if downs:
        pl.when(mode == 1)(down)
    if any(code in (2, 3) for _, _, code in ups):
        pl.when((mode == 2) | (mode == 3))(up)


VMEM = pl.BlockSpec(memory_space=pltpu.VMEM)
SMEM = pl.BlockSpec(memory_space=pltpu.SMEM)


def run_step(waves, meta, turned, tiles, here, left, right, below, down_all, up_all, halo):
    shots = here.shape[1]
    tile = here.shape[2] // 2
    codes = {code for _, _, code in waves}
    used = ([turned] if 1 in codes else []) + ([tiles] if codes & {2, 3, 4} else [])
    n_send = sends_of(waves)
    kept = (down_all, up_all) if writes_down(waves) else (up_all,)
    at = 6 - len(kept) + len(used) + len(below)
    result = pl.pallas_call(
        functools.partial(step_kernel, waves, bool(halo)),
        out_shape=[pltpu.VMEM(x.shape, BF16) for x in [here] * n_send + [*kept]],
        in_specs=[SMEM] + [VMEM] * (5 + len(used) + len(below) + len(halo)),
        out_specs=[VMEM] * (n_send + len(kept)),
        input_output_aliases={at + i: n_send + i for i in range(len(kept))},
        scratch_shapes=[
            pltpu.VMEM((6, 2 * shots, 2 * tile), BF16),
            pltpu.VMEM((6, 2 * shots, tile), F32),
        ],
        compiler_params=pltpu.CompilerParams(vmem_limit_bytes=24 << 20),
        name="step",
    )(meta, *map(resident, (here, left, right, *used, *below, down_all, up_all, *halo)))
    sends, (*down, up_all) = result[:n_send], result[n_send:]
    return *sends, *(down or [down_all]), up_all


def resident(x):
    return pltpu.with_memory_space_constraint(x, pltpu.VMEM)


def on_device(source, tile_data, tile_rows, tile_cols, tile_count):
    layers, ranges = lax.axis_size("layer"), lax.axis_size("blk")
    layer, rng = lax.axis_index("layer"), lax.axis_index("blk")
    own = source.shape[3] // tile_data.shape[3]
    first = rng * own
    meta = jnp.concatenate(
        [
            jnp.stack([layer, tile_count[0, 0], (rng > 0).astype(jnp.int32), (rng < ranges - 1).astype(jnp.int32)]),
            tile_rows[0] - first,
            tile_cols[0] - first + own,
        ]
    )
    sources = source[0]
    shots = source.shape[2] // WAVES

    def part(b):
        return lax.slice_in_dim(sources, b * shots, (b + 1) * shots, axis=1)

    def around(x, shift):
        edges = [(0, 0, 1), (2, 2, -1), (1, 3, 0), (3, 1, 0)]
        edges += [(l, l ^ 1, 0) for l in range(4, layers)]
        return lax.ppermute(x, AXES, route(edges, shift, ranges))

    def back(x):
        pairs = [(l * ranges + g, (l - 1) % layers * ranges + g) for l in range(layers) for g in range(ranges)]
        return lax.ppermute(x, AXES, pairs)

    halos = [(around(part(b), 1), around(part(b), -1)) for b in range(WAVES)]
    belows = [back(part(b)) for b in range(WAVES)]
    tiles = tile_data[0]
    turned = jnp.swapaxes(tiles, 2, 3)
    down_all, up_all = sources, jnp.zeros_like(sources)
    here = left = right = part(0)
    for waves, edges in schedule(layers):
        halo = [h for b, at, code in waves if code == 1 and at == 0 for h in halos[b]]
        below = [belows[b] for b, _, code in waves if code == 1] or belows[:1]
        *sends, down_all, up_all = run_step(
            waves, meta, turned, tiles, here, left, right, below, down_all, up_all, halo
        )
        if edges:
            sends = dict(zip((0, 1, -1), sends * (3 // len(sends))))
            got = {s: lax.ppermute(sends[s], AXES, route(edges, s, ranges)) for s in ORDER}
            here, left, right = got[0], got[1], got[-1]
    return (down_all[None], up_all[None])


def solution(mesh):
    in_specs = (
        P("layer", None, None, "blk"),
        P("layer", "blk", None, None, None),
        P("layer", "blk"),
        P("layer", "blk"),
        P("layer", "blk"),
    )
    out_specs = (P("layer", None, None, "blk"), P("layer", None, None, "blk"))
    return jax.shard_map(
        on_device, mesh=mesh, in_specs=in_specs, out_specs=out_specs, check_vma=False
    )
```
